1024 devices in a mesh: rep: 64 (over z_lo, x, core), tp: 16 (over y, z_hi).
Axes of the slice: x: 4, y: 8, z: 16 (z_hi: 2, z_lo: 8; z = z_hi * 8 + z_lo), core: 2. Of those that a mesh axis runs over, the one named last changes fastest.
Arguments:
- queries: bfloat16 [64, 4, 16384], P('rep'), may hold values from -18 to 18
- cache_keys: bfloat16 [64, 16, 16, 64, 128], P('rep', 'tp'), may hold values from -8 to 8
- cache_values: bfloat16 [64, 16, 16, 64, 128], P('rep', 'tp'), may hold values from -6 to 6
- page_table: int32 [64, 16, 16], P('rep', 'tp'), may hold values from 0 to 15, each once within a row
- lengths: int32 [64], P('rep'), may hold values from 4 to 2048, as said below
- history: bfloat16 [64, 12, 16384], P('rep', None, 'tp'), may hold values from -10 to 10
- norm_gain: float32 [16384], P('tp'), may hold values from 0.5 to 2
- draft_weight: float32 [16384, 16384], P('tp', 'rep'), may hold values from -0.1640625 to 0.1640625
- targets: int32 [64, 16], replicated, may hold values from 0 to 16383
- accepted: int32 [64], replicated, may hold values from 1 to 16, as said below
Outputs:
- attended: bfloat16 [64, 4, 16384], P('rep', None, 'tp')
- new_weight: float32 [16384, 16384], P('tp', 'rep')
The draws below stay inside these ranges and needn't reach their ends.
Inputs may be any that keep to these rules, and one draw needn't show every extreme that they name: `lengths`: some replica's sequence has length exactly 2048. `accepted`: some replica trains all 16 rows.
All inputs are finite; a program needn't handle non-finite values.
Results may differ from the reference program's by a relative error of at most 0.01.
Values may be sent and summed in bfloat16 or wider, within the bound.
A program may use at most 32 MiB of HBM per device.

```python
import math
import jax
import jax.numpy as jnp
from jax import lax

HQ = 128
KVH = 8
HD = 128
D = 16384
VOCAB = 16384
STEPS = 4
PAGE = 64
MAXP = 16
HIST = 12
ROWS = 16
KVD = 1
CP = 2
MAXLEN = 2048
N_REP = 64
N_TP = 16


def draw_queries(key, part):
    base = jax.random.truncated_normal(jax.random.fold_in(key, 11), -6.0, 6.0, (N_REP, STEPS, D), jnp.float32)
    return base.astype(jnp.bfloat16)


def draw_cache_keys(key, part):
    base = jax.random.truncated_normal(jax.random.fold_in(key, 21), -6.0, 6.0, (N_REP, N_TP, MAXP, PAGE, KVD * HD), jnp.float32)
    return base.astype(jnp.bfloat16)


def draw_history(key, part):
    shape = (N_REP, HIST, D)
    base = jax.random.truncated_normal(jax.random.fold_in(key, 31), -6.0, 6.0, shape, jnp.float32)
    return base.astype(jnp.bfloat16)


def draw_draft_weight(key, part):
    base = 3.0 * jax.random.truncated_normal(jax.random.fold_in(key, 41), -6.0, 6.0, (D, VOCAB), jnp.float32) * D ** (-0.5)
    return base


def draw_lengths(key, part):
    first, second = jax.random.split(key)
    values = jax.random.randint(first, (N_REP,), STEPS, MAXLEN + 1, dtype=jnp.int32)
    chosen = jax.random.randint(second, (), 0, N_REP, dtype=jnp.int32)
    return values.at[chosen].set(MAXLEN)


def draw_accepted(key, part):
    first, second = jax.random.split(jax.random.fold_in(key, 7))
    values = jax.random.randint(first, (N_REP,), 1, ROWS + 1, dtype=jnp.int32)
    chosen = jax.random.randint(second, (), 0, N_REP, dtype=jnp.int32)
    return values.at[chosen].set(ROWS)


def touch_ends(entries, stream_key, least, top_value):
    longest = entries.shape.index(max(entries.shape))
    spots = []
    for shift in (0, 1):
        where = [jax.random.randint(jax.random.fold_in(stream_key, axis), (), 0, length) for axis, length in enumerate(entries.shape)]
        where[longest] = (where[longest] + shift) % entries.shape[longest]
        spots.append(tuple(where))
    return entries.at[spots[0]].set(least).at[spots[1]].set(top_value)


def level_of(rng, shape, shards, low, top_value):
    def one(dim, shards_of):
        heights = jax.random.uniform(jax.random.fold_in(jax.random.fold_in(rng, 6), dim), (shards_of,), jnp.float32, low / len(shards), top_value / len(shards))
        return jnp.repeat(jnp.exp(heights), shape[dim] // shards_of).reshape((-1,) + (1,) * (len(shape) - dim - 1))

    gain = one(*shards[0])
    for cut in shards[1:]:
        gain = gain * one(*cut)
    return gain


def gaussian(own_key, extent, width, most, pieces=(), kind=jnp.bfloat16):
    array = jax.random.normal(own_key, extent, jnp.float32) * width
    if len(pieces) > 0:
        array = level_of(own_key, extent, pieces, -0.22, 0.18) * array
    return jnp.clip(array, min=-most, max=most).astype(kind)


def setup_inputs(seed: int = 0) -> dict:
    key_list = jax.random.split(jax.random.key(seed), 11)
    queries = draw_queries(jax.random.fold_in(key_list[10], 71), 0)
    cache_keys = draw_cache_keys(jax.random.fold_in(key_list[10], 71), 0)
    cache_values = gaussian(key_list[2], (N_REP, N_TP, MAXP, PAGE, KVD * HD), 1.0, 6.0, ((0, 64), (1, 16)))
    page_table = jax.vmap(lambda own: jax.random.permutation(own, MAXP))(jax.random.split(key_list[3], N_REP * N_TP)).reshape((N_REP, N_TP, MAXP)).astype(jnp.int32)
    lengths = draw_lengths(jax.random.fold_in(key_list[10], 71), 0)
    history = draw_history(jax.random.fold_in(key_list[10], 71), 0)
    norm_gain = jnp.clip(jnp.exp(math.log(2.0) - 1.3862944 * jax.random.uniform(key_list[6], (D,), jnp.float32) ** level_of(key_list[6], (D,), ((0, 16),), -0.2, 0.2)), 0.5, 2.0)
    draft_weight = draw_draft_weight(jax.random.fold_in(key_list[10], 71), 0)
    targets = touch_ends(jax.random.randint(key_list[8], (N_REP, ROWS), 0, VOCAB), jax.random.fold_in(key_list[8], 1), 0, VOCAB - 1).astype(jnp.int32)
    accepted = draw_accepted(jax.random.fold_in(key_list[10], 71), 0)
    return {"queries": queries, "cache_keys": cache_keys, "cache_values": cache_values, "page_table": page_table, "lengths": lengths, "history": history, "norm_gain": norm_gain, "draft_weight": draft_weight, "targets": targets, "accepted": accepted}


learn_rate = 0.5

def one_replica(items):
    query, key_pages, value_pages, table, length = items
    groups = N_TP // CP
    owners = jnp.arange(N_TP, dtype=jnp.int32)[:, None]

    def arrange(pages):
        picked = pages[owners, table].reshape(groups, CP, MAXP, PAGE, KVD, HD)
        return picked.transpose(0, 4, 2, 1, 3, 5).reshape(KVH, MAXLEN, HD)
    keys = arrange(key_pages).astype(jnp.float32)
    values = arrange(value_pages).astype(jnp.float32)
    position = jnp.arange(MAXLEN, dtype=jnp.int32)
    limit = length - STEPS + jnp.arange(STEPS, dtype=jnp.int32)
    valid = (position[None, :] <= limit[:, None])[:, None, None, :]
    grouped = query.astype(jnp.float32).reshape(STEPS, KVH, HQ // KVH, HD)
    scores = jnp.einsum('skgd,kpd->skgp', grouped, keys) * HD ** (-0.5)
    top = lax.optimization_barrier(jnp.max(jnp.where(valid, scores, -1e+30), axis=-1))
    expo = jnp.where(valid, jnp.exp(scores - top[..., None]), 0.0)
    total = lax.optimization_barrier(jnp.sum(expo, axis=-1))
    weighted = jnp.einsum('skgp,kpd->skgd', expo, values)
    return (weighted / total[..., None]).reshape(STEPS, D).astype(jnp.bfloat16)

def reference(queries, cache_keys, cache_values, page_table, lengths, history, norm_gain, draft_weight, targets, accepted):
    attended = lax.map(one_replica, (queries, cache_keys, cache_values, page_table, lengths))
    raw = jnp.concatenate([attended, history], axis=1)
    wide = raw.astype(jnp.float32)
    normed = wide * lax.rsqrt(lax.optimization_barrier(jnp.mean(wide * wide, axis=-1, keepdims=True)) + 1e-05) * norm_gain
    rows = normed.reshape(N_REP * ROWS, D)
    logits = jnp.dot(rows, draft_weight, precision=lax.Precision.HIGHEST, preferred_element_type=jnp.float32)
    top = lax.optimization_barrier(jnp.max(logits, axis=-1, keepdims=True))
    expo = jnp.exp(logits - top)
    probs = expo / lax.optimization_barrier(jnp.sum(expo, axis=-1, keepdims=True))
    onehot = (targets.reshape(-1)[:, None] == jnp.arange(VOCAB, dtype=jnp.int32)[None, :]).astype(jnp.float32)
    keep = (jnp.arange(ROWS, dtype=jnp.int32)[None, :] < accepted[:, None]).reshape(-1).astype(jnp.float32)
    delta = (probs - onehot) * keep[:, None]
    grad = jnp.dot(rows.T, delta, precision=lax.Precision.HIGHEST, preferred_element_type=jnp.float32)
    return (attended, draft_weight - learn_rate * grad)
```

```python
import jax
import jax.numpy as jnp
from jax import lax
from jax.experimental import pallas as pl
from jax.experimental.pallas import tpu as pltpu
from jax.sharding import PartitionSpec as P

NX, NCORE, NY, NZL = 4, 2, 8, 8
NC = NX * NCORE
FEAT = 1024
COLS = 256
HEADS = 8
STEPS = 4
HD = 128
D = 16384
LEARN_RATE = 0.5
EPS = 1e-5
F32 = jnp.float32
BF16 = jnp.bfloat16
HROWS, AROWS = 96, 32


def remote(src, dst, send, recv, where):
    return pltpu.make_async_remote_copy(
        src_ref=src,
        dst_ref=dst,
        send_sem=send,
        recv_sem=recv,
        device_id=where,
        device_id_type=pl.DeviceIdType.MESH,
    )


def split_bf16(value):
    high = value.astype(BF16)
    return high, (value - high.astype(F32)).astype(BF16)


def dot(a, b):
    return jnp.dot(a, b, preferred_element_type=F32)


def body(
    q_hbm, k_hbm, v_hbm, table, length, hist, gain, w_hbm, targets, accepted,
    att_out, w_out,
    qv, kv, vv, wv, q32, part, px_send, px_recv, blk,
    r8, r4, ra, f4, xh, xa, xt, whi, wlo, gcol, pacc,
    tmp, tk, tcol_h, tcol_a,
    ysh, ysa, yrh, yra, ssh, ssa, srh, sra,
    zsh, zsa, zrh, zra, zssh, zssa, zrsh, zrsa,
    lgh, lga, stzh, stza, stxh, stxa, stch, stca,
    eh, ea, sch, sca, dd,
    load_sem, px_sem, gz_sem, gx_sem, gc_sem, y_sem, z_sem, sz_sem, sx_sem, sc_sem, e_sem, a_sem,
):
    rep = lax.axis_index("rep")
    tp = lax.axis_index("tp")
    core = lax.rem(rep, 2)
    x = lax.rem(rep // 2, NX)
    zl = rep // NC
    zh = lax.rem(tp, 2)
    y = tp // 2
    cc = x * NCORE + core

    def at(zl_=None, x_=None, core_=None, y_=None, zh_=None):
        r = ((zl if zl_ is None else zl_) * NX + (x if x_ is None else x_)) * NCORE + (core if core_ is None else core_)
        t = (y if y_ is None else y_) * 2 + (zh if zh_ is None else zh_)
        return (r, t)

    z_peers = [(j, at(zl_=lax.rem(zl + j, NZL))) for j in range(1, NZL)]
    x_peers = [(j, at(x_=lax.rem(x + j, NX))) for j in range(1, NX)]
    c_peer = at(core_=1 - core)
    y_peers = [(j, lax.rem(y + j, NY)) for j in range(1, NY)]
    h_peer = at(zh_=1 - zh)

    barrier = pltpu.get_barrier_semaphore()
    everyone = [w for _, w in z_peers] + [w for _, w in x_peers] + [c_peer] + [at(y_=t) for _, t in y_peers] + [h_peer]
    for where in everyone:
        pl.semaphore_signal(barrier, inc=1, device_id=where, device_id_type=pl.DeviceIdType.MESH)

    group = tp // 2
    loads = [
        pltpu.make_async_copy(q_hbm.at[0, :, pl.ds(pl.multiple_of(group * 2048, 2048), 2048)], qv, load_sem.at[0]),
        pltpu.make_async_copy(k_hbm, kv, load_sem.at[1]),
        pltpu.make_async_copy(v_hbm, vv, load_sem.at[2]),
        pltpu.make_async_copy(w_hbm, wv, load_sem.at[3]),
    ]
    for load in loads:
        load.start()

    tmp[...] = jnp.zeros_like(tmp)
    part[...] = jnp.zeros_like(part)

    h32 = hist[...].astype(F32)
    r8[cc, zl] = h32[0:8].astype(BF16)
    r4[cc, zl] = h32[8:12].astype(BF16)

    loads[0].wait()
    loads[1].wait()
    loads[2].wait()
    for h in range(16):
        q32[h * STEPS : (h + 1) * STEPS, :] = qv[:, h * HD : (h + 1) * HD].astype(F32)
    scores = lax.dot_general(
        q32[...].astype(BF16), kv[...], (((1,), (1,)), ((), ())), preferred_element_type=F32
    ) * (HD ** -0.5)
    lane = lax.broadcasted_iota(jnp.int32, (64, 1024), 1)
    row = lax.broadcasted_iota(jnp.int32, (64, 1024), 0)
    page = lane // 64
    logical = jnp.zeros((64, 1024), jnp.int32)
    for j in range(16):
        logical = jnp.where(page == table[0, j], j, logical)
    position = (logical * 2 + zh) * 64 + lax.rem(lane, 64)
    valid = position <= length[0] - STEPS + lax.rem(row, STEPS)
    top = jnp.max(jnp.where(valid, scores, -1e30), axis=-1, keepdims=True)
    expo = jnp.where(valid, jnp.exp(scores - top), 0.0)
    total = jnp.sum(expo, axis=-1, keepdims=True)
    e_high, e_low = split_bf16(expo)
    acc = dot(e_high, vv[...]) + dot(e_low, vv[...])
    part[0:64, :] = acc
    tmp[0:64, :] = jnp.broadcast_to(top, (64, 128))
    tmp[64:128, :] = jnp.broadcast_to(total, (64, 128))
    stat_rows = jnp.transpose(tmp[...])
    other = pl.multiple_of((1 - zh) * 32, 32)
    px_send[0:32, :] = part[pl.ds(other, 32), :]
    px_send[32:40, :] = stat_rows[0:8, :]

    pl.semaphore_wait(barrier, len(everyone))
    px = remote(px_send, px_recv, px_sem.at[0], px_sem.at[1], h_peer)
    px.start()

    def gather(buf, i):
        z = [
            remote(buf.at[cc, zl], buf.at[cc, zl], gz_sem.at[i, 0, j], gz_sem.at[i, 1, j], where)
            for j, where in z_peers
        ]
        xs = [
            remote(buf.at[cc], buf.at[cc], gx_sem.at[i, 0, j], gx_sem.at[i, 1, j], where)
            for j, where in x_peers
        ]
        cs = []
        for j in range(NX):
            k = lax.rem(x + j, NX) * NCORE + core
            cs.append(remote(buf.at[k], buf.at[k], gc_sem.at[i, 0, j], gc_sem.at[i, 1, j], c_peer))
        return z, xs, cs

    def start(copies):
        for copy in copies:
            copy.start()

    def wait(copies):
        for copy in copies:
            copy.wait()

    g8, g4, ga = gather(r8, 0), gather(r4, 1), gather(ra, 2)
    start(g8[0] + g4[0])

    loads[3].wait()

    def make_w(b, _):
        rows = pl.ds(pl.multiple_of(b * 128, 128), 128)
        g = jnp.transpose(jnp.broadcast_to(gain[0:1, rows], (128, 128)))
        gcol[rows, :] = g
        w = wv[rows, :] * jnp.concatenate([g, g], axis=1)
        high, low = split_bf16(w)
        whi[rows, :] = high
        wlo[rows, :] = low
        return 0

    lax.fori_loop(0, 8, make_w, 0)

    acc_row = accepted[...].astype(F32)
    ri = lax.broadcasted_iota(jnp.int32, (64, 64), 0)
    li = lax.broadcasted_iota(jnp.int32, (64, 64), 1)
    acc_col = jnp.sum(jnp.where(ri == li, jnp.broadcast_to(acc_row, (64, 64)), 0.0), axis=1, keepdims=True)
    ii = lax.broadcasted_iota(jnp.int32, (64, 16), 1).astype(F32)
    tk[...] = jnp.where(ii < acc_col, targets[...].astype(F32), -1.0)

    def target_cols(n, zl_of, i_of, out):
        rho = lax.broadcasted_iota(jnp.int32, (n, 64), 0)
        rep_lane = lax.broadcasted_iota(jnp.int32, (n, 64), 1)
        rho16 = lax.broadcasted_iota(jnp.int32, (n, 16), 0)
        lane16 = lax.broadcasted_iota(jnp.int32, (n, 16), 1)

        def one(c, _):
            pick = (rep_lane == zl_of(rho) * NC + c).astype(F32)
            rows = jnp.dot(pick, tk[...], precision=lax.Precision.HIGHEST, preferred_element_type=F32)
            col = jnp.sum(jnp.where(lane16 == i_of(rho16), rows, 0.0), axis=1, keepdims=True)
            out[c] = jnp.broadcast_to(col, (n, 128))
            return 0

        lax.fori_loop(0, NY, one, 0)

    target_cols(
        HROWS,
        lambda p: jnp.where(p < 64, p // 8, (p - 64) // 4),
        lambda p: jnp.where(p < 64, 4 + lax.rem(p, 8), 12 + lax.rem(p, 4)),
        tcol_h,
    )
    target_cols(AROWS, lambda p: p // 4, lambda p: lax.rem(p, 4), tcol_a)

    wait(g8[0] + g4[0])
    start(g8[1] + g4[1])

    px.wait()
    tmp[0:64, :] = jnp.broadcast_to(stat_rows[0:1, :], (64, 128))
    tmp[64:128, :] = jnp.broadcast_to(px_recv[32:33, :], (64, 128))
    tmp[...] = jnp.transpose(tmp[...])
    mine = pl.multiple_of(zh * 32, 32)
    top_a = tmp[pl.ds(mine, 32), 0:1]
    sum_a = tmp[pl.ds(mine + 64, 32), 0:1]
    top_b = tmp[pl.ds(mine, 32), 64:65]
    sum_b = tmp[pl.ds(mine + 64, 32), 64:65]
    top_ab = jnp.maximum(top_a, top_b)
    left = jnp.exp(top_a - top_ab)
    right = jnp.exp(top_b - top_ab)
    joined = (part[pl.ds(mine, 32), :] * left + px_recv[0:32, :] * right) / (sum_a * left + sum_b * right)
    part[0:32, :] = joined
    for h in range(HEADS):
        blk[:, h * HD : (h + 1) * HD] = part[h * STEPS : (h + 1) * STEPS, :]
    own = blk[...].astype(BF16)
    ra[cc, zl] = own
    att_out[0] = own
    start(ga[0])

    wait(g8[1] + g4[1])
    start(g8[2] + g4[2])
    wait(ga[0])
    start(ga[1])

    def row_form(col, n):
        tmp[0:n, :] = jnp.broadcast_to(col, (n, 128))
        return jnp.transpose(tmp[...])[0:8, :]

    wait(g8[2] + g4[2])

    def prep_h(c, _):
        v8 = r8[c].astype(F32).reshape(64, FEAT)
        base = pl.multiple_of(c * HROWS, 32)
        for j in range(4):
            f4[j, 0:4, :] = r4[c, 2 * j].astype(F32)
            f4[j, 4:8, :] = r4[c, 2 * j + 1].astype(F32)
        v4 = f4[...].reshape(32, FEAT)
        xh[pl.ds(base, 64), :] = v8.astype(BF16)
        xh[pl.ds(pl.multiple_of(base + 64, 32), 32), :] = v4.astype(BF16)
        tmp[0:64, :] = jnp.broadcast_to(jnp.sum(v8 * v8, axis=1, keepdims=True), (64, 128))
        tmp[64:96, :] = jnp.broadcast_to(jnp.sum(v4 * v4, axis=1, keepdims=True), (32, 128))
        ssh[c] = jnp.transpose(tmp[...])[0:8, :]
        return 0

    lax.fori_loop(0, NY, prep_h, 0)
    pacc[...] = dot(xh[...], whi[...]) + dot(xh[...], wlo[...])

    def pack_h(c, _):
        ysh[c] = pacc[pl.ds(pl.multiple_of(c * HROWS, 32), HROWS), :].astype(BF16)
        return 0

    lax.fori_loop(0, NY, pack_h, 0)

    def scatter(i, send, ss_send, recv, ss_recv):
        copies = []
        for j, t in y_peers:
            where = at(y_=t)
            copies.append(remote(ss_send.at[t], ss_recv.at[y], y_sem.at[i, 0, j], y_sem.at[i, 1, j], where))
            copies.append(remote(send.at[t], recv.at[y], y_sem.at[i, 2, j], y_sem.at[i, 3, j], where))
        return copies

    rs_h = scatter(0, ysh, ssh, yrh, srh)
    rs_a = scatter(1, ysa, ssa, yra, sra)
    start(rs_h)

    wait(ga[1])
    start(ga[2])

    def transpose_x(src, off, count):
        def one(b, _):
            rows = pl.ds(pl.multiple_of(b * 128, 128), 128)
            lanes = pl.ds(pl.multiple_of(off + b * 128, 128), 128)
            xt[:, lanes] = jnp.transpose(src[rows, :].astype(F32)).astype(BF16)
            return 0

        lax.fori_loop(0, count, one, 0)

    wait(ga[2])

    def prep_a(c, _):
        for j in range(4):
            f4[j, 0:4, :] = ra[c, 2 * j].astype(F32)
            f4[j, 4:8, :] = ra[c, 2 * j + 1].astype(F32)
        v4 = f4[...].reshape(32, FEAT)
        xa[pl.ds(pl.multiple_of(c * AROWS, 32), 32), :] = v4.astype(BF16)
        ssa[c] = row_form(jnp.sum(v4 * v4, axis=1, keepdims=True), AROWS)
        return 0

    lax.fori_loop(0, NY, prep_a, 0)
    pacc[0:256, :] = dot(xa[...], whi[...]) + dot(xa[...], wlo[...])

    def pack_a(c, _):
        ysa[c] = pacc[pl.ds(pl.multiple_of(c * AROWS, 32), AROWS), :].astype(BF16)
        return 0

    lax.fori_loop(0, NY, pack_a, 0)
    start(rs_a)
    transpose_x(xh, 0, 6)
    transpose_x(xa, 768, 2)

    def exchange(i, zs, zss, zr, zrs):
        return [
            remote(zss, zrs, z_sem.at[i, 0], z_sem.at[i, 1], h_peer),
            remote(zs, zr, z_sem.at[i, 2], z_sem.at[i, 3], h_peer),
        ]

    zx_h = exchange(0, zsh, zssh, zrh, zrsh)
    zx_a = exchange(1, zsa, zssa, zra, zrsa)

    def sum_y(copies, send, ss_send, recv, ss_recv, zs, zss, lg, zx):
        wait(copies)
        lg[...] = send[y].astype(F32)
        total = ss_send[y]
        for j in range(1, NY):
            t = lax.rem(y + j, NY)
            lg[...] += recv[t].astype(F32)
            total = total + ss_recv[t]
        zs[...] = lg[...].astype(BF16)
        zss[...] = total
        start(zx)

    sum_y(rs_h, ysh, ssh, yrh, srh, zsh, zssh, lgh, zx_h)
    sum_y(rs_a, ysa, ssa, yra, sra, zsa, zssa, lga, zx_a)

    def column(row_ref_value, n):
        return jnp.transpose(jnp.broadcast_to(row_ref_value, (128, 128)))[0:n, :]

    def gather_y(i, buf, sem):
        return [
            remote(buf.at[y], buf.at[y], sem.at[i, 0, j], sem.at[i, 1, j], at(y_=t)) for j, t in y_peers
        ]

    def stats_copies(i, stz, stx, stc):
        z = [remote(stz.at[zl], stz.at[zl], sz_sem.at[i, 0, j], sz_sem.at[i, 1, j], w) for j, w in z_peers]
        xs = [remote(stx.at[x], stx.at[x], sx_sem.at[i, 0, j], sx_sem.at[i, 1, j], w) for j, w in x_peers]
        c = [remote(stc.at[core], stc.at[core], sc_sem.at[i, 0], sc_sem.at[i, 1], c_peer)]
        return z, xs, c

    st_h = stats_copies(0, stzh, stxh, stch)
    st_a = stats_copies(1, stza, stxa, stca)
    e_h, e_a = gather_y(0, eh, e_sem), gather_y(1, ea, e_sem)
    s_h, s_a = gather_y(0, sch, a_sem), gather_y(1, sca, a_sem)

    def logits(n, zx, zr, zrs, zss, lg, stz, st, e_buf, e_copies):
        wait(zx)
        ss = zss[...] + zrs[...]
        scale_row = lax.rsqrt(ss / D + EPS)
        scale = column(scale_row[0:1, :], n)
        value = (lg[...] + zr[...].astype(F32)) * jnp.concatenate([scale, scale], axis=1)
        top_l = jnp.max(value, axis=1, keepdims=True)
        ex = jnp.exp(value - top_l)
        sum_l = jnp.sum(ex, axis=1, keepdims=True)
        e_buf[y] = ex.astype(BF16)
        m_row = row_form(top_l, n)
        l_row = row_form(sum_l, n)
        stz[zl, 0:4, :] = m_row[0:4, :]
        stz[zl, 4:8, :] = l_row[0:4, :]
        start(st[0])
        start(e_copies)
        return scale_row, m_row

    def join(buf, n):
        m = buf[0, 0:4, :]
        for j in range(1, n):
            m = jnp.maximum(m, buf[j, 0:4, :])
        total = buf[0, 4:8, :] * jnp.exp(buf[0, 0:4, :] - m)
        for j in range(1, n):
            total = total + buf[j, 4:8, :] * jnp.exp(buf[j, 0:4, :] - m)
        return m, total

    def pass_on(copies, buf, n, out, slot, nxt):
        wait(copies)
        m, total = join(buf, n)
        out[slot, 0:4, :] = m
        out[slot, 4:8, :] = total
        start(nxt)

    def finish(copies, stc, sc, scale_row, m_row, nxt):
        wait(copies)
        m, total = join(stc, 2)
        sc[y, 0:4, :] = jnp.exp(m_row[0:4, :] - m) / total
        sc[y, 4:8, :] = scale_row[0:4, :]
        start(nxt)

    row_h = logits(HROWS, zx_h, zrh, zrsh, zssh, lgh, stzh, st_h, eh, e_h)
    row_a = logits(AROWS, zx_a, zra, zrsa, zssa, lga, stza, st_a, ea, e_a)
    pass_on(st_h[0], stzh, NZL, stxh, x, st_h[1])
    pass_on(st_a[0], stza, NZL, stxa, x, st_a[1])
    pass_on(st_h[1], stxh, NX, stch, core, st_h[2])
    pass_on(st_a[1], stxa, NX, stca, core, st_a[2])
    finish(st_h[2], stch, sch, row_h[0], row_h[1], s_h)
    finish(st_a[2], stca, sca, row_a[0], row_a[1], s_a)

    labels = (lax.broadcasted_iota(jnp.int32, (1, COLS), 1) + rep * COLS).astype(F32)

    def deltas(n, off, e_buf, sc, tcol):
        def one(c, _):
            s = column(sc[c, 0:1, :], n)
            scale = column(sc[c, 4:5, :], n)
            t = tcol[c]
            t2 = jnp.concatenate([t, t], axis=1)
            p = e_buf[c].astype(F32) * jnp.concatenate([s, s], axis=1)
            delta = jnp.where(t2 >= 0.0, p - jnp.where(t2 == labels, 1.0, 0.0), 0.0)
            delta = delta * jnp.concatenate([scale, scale], axis=1)
            dd[pl.ds(pl.multiple_of(off + c * n, 32), n), :] = delta.astype(BF16)
            return 0

        lax.fori_loop(0, NY, one, 0)

    wait(e_h)
    wait(s_h)
    deltas(HROWS, 0, eh, sch, tcol_h)
    wait(e_a)
    wait(s_a)
    deltas(AROWS, 768, ea, sca, tcol_a)

    def update(b, _):
        rows = pl.ds(pl.multiple_of(b * 256, 256), 256)
        grad = dot(xt[rows, :], dd[...])
        g = gcol[rows, :] * LEARN_RATE
        w_out[rows, :] = wv[rows, :] - jnp.concatenate([g, g], axis=1) * grad
        return 0

    lax.fori_loop(0, 4, update, 0)


def on_device(queries, cache_keys, cache_values, page_table, lengths, history, norm_gain, draft_weight, targets, accepted):
    vmem = pl.BlockSpec(memory_space=pltpu.VMEM)
    smem = pl.BlockSpec(memory_space=pltpu.SMEM)
    hbm = pl.BlockSpec(memory_space=pl.ANY)
    V = pltpu.VMEM
    dma = pltpu.SemaphoreType.DMA
    attended, new_weight = pl.pallas_call(
        body,
        out_shape=(
            jax.ShapeDtypeStruct((1, STEPS, FEAT), BF16),
            jax.ShapeDtypeStruct((FEAT, COLS), F32),
        ),
        in_specs=[hbm, hbm, hbm, smem, smem, vmem, vmem, hbm, vmem, vmem],
        out_specs=(vmem, vmem),
        scratch_shapes=[
            V((STEPS, 2048), BF16), V((1024, HD), BF16), V((1024, HD), BF16), V((FEAT, COLS), F32),
            V((64, HD), F32), V((64, HD), F32), V((40, HD), F32), V((40, HD), F32), V((STEPS, FEAT), F32),
            V((NC, NZL, 8, FEAT), BF16), V((NC, NZL, 4, FEAT), BF16), V((NC, NZL, 4, FEAT), BF16),
            V((4, 8, FEAT), F32), V((768, FEAT), BF16), V((256, FEAT), BF16), V((FEAT, 1024), BF16),
            V((FEAT, COLS), BF16), V((FEAT, COLS), BF16), V((FEAT, 128), F32), V((768, COLS), F32),
            V((128, 128), F32), V((64, 16), F32), V((NY, HROWS, 128), F32), V((NY, AROWS, 128), F32),
            V((NY, HROWS, COLS), BF16), V((NY, AROWS, COLS), BF16), V((NY, HROWS, COLS), BF16), V((NY, AROWS, COLS), BF16),
            V((NY, 8, 128), F32), V((NY, 8, 128), F32), V((NY, 8, 128), F32), V((NY, 8, 128), F32),
            V((HROWS, COLS), BF16), V((AROWS, COLS), BF16), V((HROWS, COLS), BF16), V((AROWS, COLS), BF16),
            V((8, 128), F32), V((8, 128), F32), V((8, 128), F32), V((8, 128), F32),
            V((HROWS, COLS), F32), V((AROWS, COLS), F32),
            V((NZL, 8, 128), F32), V((NZL, 8, 128), F32), V((NX, 8, 128), F32), V((NX, 8, 128), F32),
            V((2, 8, 128), F32), V((2, 8, 128), F32),
            V((NY, HROWS, COLS), BF16), V((NY, AROWS, COLS), BF16), V((NY, 8, 128), F32), V((NY, 8, 128), F32),
            V((1024, COLS), BF16),
            dma((4,)), dma((2,)), dma((3, 2, 8)), dma((3, 2, 4)), dma((3, 2, 4)), dma((2, 4, 8)), dma((2, 4)),
            dma((2, 2, 8)), dma((2, 2, 4)), dma((2, 2)), dma((2, 2, 8)), dma((2, 2, 8)),
        ],
        compiler_params=pltpu.CompilerParams(collective_id=0, has_side_effects=True, vmem_limit_bytes=48 * 1024 * 1024),
        name="decode_draft_step",
    )(
        queries,
        cache_keys.reshape(1024, HD),
        cache_values.reshape(1024, HD),
        page_table.reshape(1, 16),
        lengths,
        history.reshape(12, FEAT),
        norm_gain.reshape(1, FEAT),
        draft_weight,
        targets,
        accepted.reshape(1, 64),
    )
    return attended, new_weight


def solution(mesh):
    return jax.shard_map(
        on_device,
        mesh=mesh,
        in_specs=(
            P("rep", None, None),
            P("rep", "tp", None, None, None),
            P("rep", "tp", None, None, None),
            P("rep", "tp", None),
            P("rep"),
            P("rep", None, "tp"),
            P("tp"),
            P("tp", "rep"),
            P(),
            P(),
        ),
        out_specs=(P("rep", None, "tp"), P("tp", "rep")),
        check_vma=False,
    )
```

```python
import jax
import jax.numpy as jnp
from jax import lax
from jax.experimental import pallas as pl
from jax.experimental.pallas import tpu as pltpu
from jax.sharding import PartitionSpec as P

NX, NCORE, NY, NZL = 4, 2, 8, 8
NC = NX * NCORE
FEAT = 1024
COLS = 256
HEADS = 8
STEPS = 4
HD = 128
D = 16384
LEARN_RATE = 0.5
EPS = 1e-5
F32 = jnp.float32
BF16 = jnp.bfloat16
HROWS, AROWS = 96, 32


def remote(src, dst, send, recv, where):
    return pltpu.make_async_remote_copy(
        src_ref=src,
        dst_ref=dst,
        send_sem=send,
        recv_sem=recv,
        device_id=where,
        device_id_type=pl.DeviceIdType.MESH,
    )


def split_bf16(value):
    high = value.astype(BF16)
    return high, (value - high.astype(F32)).astype(BF16)


def dot(a, b):
    return jnp.dot(a, b, preferred_element_type=F32)


def body(
    q_hbm, k_hbm, v_hbm, table_hbm, length, hist_hbm, gain_hbm, w_hbm, targets_hbm, accepted_hbm,
    att_out, w_out,
    table, hist, gain, targets, accepted,
    qv, kv, vv, wv, q32, part, px_send, px_recv, blk,
    r8, r4, ra, f4, xr, xt, whi, wlo, gcol, pacc,
    tmp, tmp2, tk, tcol,
    ysh, ysa, yrh, yra, ssh, ssa, srh, sra,
    zsh, zsa, zrh, zra, zssh, zssa, zrsh, zrsa,
    lg, stz, stp, stc, eb, sc, dd,
    load_sem, px_sem, gz_sem, gx_sem, gc_sem, y_sem, z_sem, sz_sem, sp_sem, sc_sem, e_sem, a_sem,
):
    rep = lax.axis_index("rep")
    tp = lax.axis_index("tp")
    core = lax.rem(rep, 2)
    x = lax.rem(rep // 2, NX)
    zl = rep // NC
    zh = lax.rem(tp, 2)
    y = tp // 2
    cc = x * NCORE + core

    def at(zl_=None, x_=None, core_=None, y_=None, zh_=None):
        r = ((zl if zl_ is None else zl_) * NX + (x if x_ is None else x_)) * NCORE + (core if core_ is None else core_)
        t = (y if y_ is None else y_) * 2 + (zh if zh_ is None else zh_)
        return (r, t)

    half = zl // 4
    near = [half * 4 + lax.rem(lax.rem(zl, 4) + j, 4) for j in range(1, 4)]
    far = [(1 - half) * 4 + lax.rem(lax.rem(zl, 4) + j, 4) for j in range(4)]
    z_peers = [(j, at(zl_=t)) for j, t in enumerate(near + far)]
    x_peers = [(j, at(x_=lax.rem(x + j, NX))) for j in range(1, NX)]
    plane = [
        (i, j, at(x_=lax.rem(x + i, NX), y_=lax.rem(y + j, NY)))
        for i in range(NX)
        for j in range(NY)
        if i or j
    ]
    c_peer = at(core_=1 - core)
    y_peers = [(j, lax.rem(y + j, NY)) for j in range(1, NY)]
    h_peer = at(zh_=1 - zh)

    barrier = pltpu.get_barrier_semaphore()
    everyone = [h_peer] + [w for _, w in z_peers] + [w for _, _, w in plane] + [c_peer]
    for where in everyone:
        pl.semaphore_signal(barrier, inc=1, device_id=where, device_id_type=pl.DeviceIdType.MESH)

    group = tp // 2
    loads = [
        pltpu.make_async_copy(src, dst, load_sem.at[i])
        for i, (src, dst) in enumerate(
            [
                (q_hbm.at[0, :, pl.ds(pl.multiple_of(group * 2048, 2048), 2048)], qv),
                (k_hbm, kv),
                (table_hbm, table),
                (v_hbm, vv),
                (hist_hbm, hist),
                (gain_hbm, gain),
                (w_hbm, wv),
                (targets_hbm, targets),
                (accepted_hbm, accepted),
            ]
        )
    ]
    for load in loads:
        load.start()

    def start(copies):
        for copy in copies:
            copy.start()

    def wait(copies):
        for copy in copies:
            copy.wait()

    tmp[...] = jnp.zeros_like(tmp)
    tmp2[...] = jnp.zeros_like(tmp2)

    wait(loads[0:3])
    lane = lax.broadcasted_iota(jnp.int32, (8, 1024), 1)
    page = lane // 64
    logical = jnp.zeros((8, 1024), jnp.int32)
    for j in range(16):
        logical = jnp.where(page == table[0, j], j, logical)
    position = (logical * 2 + zh) * 64 + lax.rem(lane, 64)
    row = lax.broadcasted_iota(jnp.int32, (8, 1024), 0)
    valid8 = position <= length[0] - STEPS + lax.rem(row, STEPS)
    bias = jnp.where(valid8, 0.0, -1e30)
    for h in range(16):
        q32[h * STEPS : (h + 1) * STEPS, :] = qv[:, h * HD : (h + 1) * HD].astype(F32)
    scores = lax.dot_general(
        q32[...].astype(BF16), kv[...], (((1,), (1,)), ((), ())), preferred_element_type=F32
    ) * (HD ** -0.5)
    valid = jnp.concatenate([bias] * 8, axis=0) == 0.0
    top = jnp.max(jnp.where(valid, scores, -1e30), axis=-1, keepdims=True)
    expo = jnp.where(valid, jnp.exp(scores - top), 0.0)
    total = jnp.sum(expo, axis=-1, keepdims=True)
    e_high, e_low = split_bf16(expo)
    tmp[0:64, :] = jnp.broadcast_to(top, (64, 128))
    tmp[64:128, :] = jnp.broadcast_to(total, (64, 128))
    stat_rows = jnp.transpose(tmp[...])
    loads[3].wait()
    part[...] = dot(e_high, vv[...]) + dot(e_low, vv[...])
    other = pl.multiple_of((1 - zh) * 32, 32)
    px_send[0:32, :] = part[pl.ds(other, 32), :]
    px_send[32:40, :] = stat_rows[0:8, :]

    loads[4].wait()
    h32 = hist[...].astype(F32)
    r8[cc, zl] = h32[0:8].astype(BF16)
    r4[cc, zl] = h32[8:12].astype(BF16)

    pl.semaphore_wait(barrier, len(everyone))
    px = remote(px_send, px_recv, px_sem.at[0], px_sem.at[1], h_peer)
    px.start()

    def gather(buf, i):
        z = [
            remote(buf.at[cc, zl], buf.at[cc, zl], gz_sem.at[i, 0, j], gz_sem.at[i, 1, j], where)
            for j, where in z_peers
        ]

        def piece(k, h):
            return buf.at[k, pl.ds(h * 4, 4)]

        xs, cs = [], []
        for slot, h in ((0, half), (1, 1 - half)):
            xs.append(
                [
                    remote(piece(cc, h), piece(cc, h), gx_sem.at[i, slot, 0, j], gx_sem.at[i, slot, 1, j], where)
                    for j, where in x_peers
                ]
            )
            one = []
            for j in range(NX):
                k = lax.rem(x + j, NX) * NCORE + core
                one.append(remote(piece(k, h), piece(k, h), gc_sem.at[i, slot, 0, j], gc_sem.at[i, slot, 1, j], c_peer))
            cs.append(one)
        return z[0:3], z[3:7], xs, cs

    g8, g4, ga = gather(r8, 0), gather(r4, 1), gather(ra, 2)
    start(g8[0] + g4[0] + g8[1] + g4[1])

    wait(loads[5:7])

    def make_w(b, _):
        rows = pl.ds(pl.multiple_of(b * 128, 128), 128)
        g = jnp.transpose(jnp.broadcast_to(gain[0:1, rows], (128, 128)))
        gcol[rows, :] = g
        w = wv[rows, :] * jnp.concatenate([g, g], axis=1)
        high, low = split_bf16(w)
        whi[rows, :] = high
        wlo[rows, :] = low
        return 0

    lax.fori_loop(0, 8, make_w, 0)

    wait(g8[0] + g4[0])
    start(g8[2][0] + g4[2][0])

    tmp[0:64, :] = jnp.broadcast_to(stat_rows[0:1, :], (64, 128))
    px.wait()
    tmp[64:128, :] = jnp.broadcast_to(px_recv[32:33, :], (64, 128))
    tmp[...] = jnp.transpose(tmp[...])
    mine = pl.multiple_of(zh * 32, 32)
    top_a = tmp[pl.ds(mine, 32), 0:1]
    sum_a = tmp[pl.ds(mine + 64, 32), 0:1]
    top_b = tmp[pl.ds(mine, 32), 64:65]
    sum_b = tmp[pl.ds(mine + 64, 32), 64:65]
    top_ab = jnp.maximum(top_a, top_b)
    left = jnp.exp(top_a - top_ab)
    right = jnp.exp(top_b - top_ab)
    joined = (part[pl.ds(mine, 32), :] * left + px_recv[0:32, :] * right) / (sum_a * left + sum_b * right)
    part[0:32, :] = joined
    for h in range(HEADS):
        blk[:, h * HD : (h + 1) * HD] = part[h * STEPS : (h + 1) * STEPS, :]
    own = blk[...].astype(BF16)
    ra[cc, zl] = own
    start(ga[0] + ga[1])
    att_out[0] = own

    wait(g8[1] + g4[1])
    start(g8[2][1] + g4[2][1])

    wait(loads[7:9])
    ii = lax.broadcasted_iota(jnp.int32, (16, 64), 0)
    tk[...] = jnp.where(ii < accepted[...], targets[...], -1).astype(F32)
    rho = lax.broadcasted_iota(jnp.int32, (128, 64), 0)
    rep_lane = lax.broadcasted_iota(jnp.int32, (128, 64), 1)
    zl_of = jnp.where(rho < 64, rho // 8, jnp.where(rho < 96, (rho - 64) // 4, (rho - 96) // 4))
    rho16 = lax.broadcasted_iota(jnp.int32, (128, 16), 0)
    lane16 = lax.broadcasted_iota(jnp.int32, (128, 16), 1)
    i_of = jnp.where(rho16 < 64, 4 + lax.rem(rho16, 8), jnp.where(rho16 < 96, 12, 0) + lax.rem(rho16, 4))

    def target_cols(c, _):
        pick = (rep_lane == zl_of * NC + c).astype(F32)
        rows = lax.dot_general(
            pick, tk[...], (((1,), (1,)), ((), ())), precision=lax.Precision.HIGHEST, preferred_element_type=F32
        )
        col = jnp.sum(jnp.where(lane16 == i_of, rows, 0.0), axis=1, keepdims=True)
        tcol[c] = jnp.broadcast_to(col, (128, 128))
        return 0

    lax.fori_loop(0, NY, target_cols, 0)

    wait(g8[2][0] + g4[2][0])
    start(g8[3][0] + g4[3][0])
    wait(g8[2][1] + g4[2][1])
    start(g8[3][1] + g4[3][1])

    def narrow_rows(buf, c):
        for j in range(4):
            f4[j, 0:4, :] = buf[c, 2 * j].astype(F32)
            f4[j, 4:8, :] = buf[c, 2 * j + 1].astype(F32)
        return f4[...].reshape(32, FEAT)

    wait(g8[3][0] + g4[3][0] + g8[3][1] + g4[3][1])

    def prep_h(c, _):
        v8 = r8[c].astype(F32).reshape(64, FEAT)
        v4 = narrow_rows(r4, c)
        xr[c, 0:64, :] = v8.astype(BF16)
        xr[c, 64:96, :] = v4.astype(BF16)
        tmp[0:64, :] = jnp.broadcast_to(jnp.sum(v8 * v8, axis=1, keepdims=True), (64, 128))
        tmp[64:96, :] = jnp.broadcast_to(jnp.sum(v4 * v4, axis=1, keepdims=True), (32, 128))
        tmp[96:128, :] = jnp.zeros((32, 128), F32)
        ssh[c] = jnp.transpose(tmp[...])[0:1, :]
        return 0

    lax.fori_loop(0, NY, prep_h, 0)
    wait(ga[0])
    start(ga[2][0])
    wait(ga[1])
    start(ga[2][1])

    rows_h = xr[:, 0:HROWS, :].reshape(NY * HROWS, FEAT)
    pacc[...] = dot(rows_h, whi[...]) + dot(rows_h, wlo[...])

    def pack_h(c, _):
        ysh[c] = pacc[pl.ds(pl.multiple_of(c * HROWS, 32), HROWS), :].astype(BF16)
        return 0

    lax.fori_loop(0, NY, pack_h, 0)

    def scatter(i, send, ss_send, recv, ss_recv):
        copies = []
        for j, t in y_peers:
            where = at(y_=t)
            copies.append(remote(ss_send.at[t], ss_recv.at[y], y_sem.at[i, 0, j], y_sem.at[i, 1, j], where))
            copies.append(remote(send.at[t], recv.at[y], y_sem.at[i, 2, j], y_sem.at[i, 3, j], where))
        return copies

    rs_h = scatter(0, ysh, ssh, yrh, srh)
    rs_a = scatter(1, ysa, ssa, yra, sra)
    start(rs_h)

    wait(ga[2][0] + ga[2][1])
    start(ga[3][0] + ga[3][1])
    wait(ga[3][0] + ga[3][1])

    def prep_a(c, _):
        v4 = narrow_rows(ra, c)
        xr[c, 96:128, :] = v4.astype(BF16)
        tmp2[96:128, :] = jnp.broadcast_to(jnp.sum(v4 * v4, axis=1, keepdims=True), (32, 128))
        ssa[c] = jnp.transpose(tmp2[...])[0:1, :]
        return 0

    lax.fori_loop(0, NY, prep_a, 0)
    rows_a = xr[:, HROWS:128, :].reshape(NY * AROWS, FEAT)
    pacc[0:256, :] = dot(rows_a, whi[...]) + dot(rows_a, wlo[...])

    def pack_a(c, _):
        ysa[c] = pacc[pl.ds(pl.multiple_of(c * AROWS, 32), AROWS), :].astype(BF16)
        return 0

    lax.fori_loop(0, NY, pack_a, 0)
    start(rs_a)

    def transpose_x(c, _):
        lanes = pl.ds(pl.multiple_of(c * 128, 128), 128)
        xt[:, lanes] = jnp.transpose(xr[c].astype(F32)).astype(BF16)
        return 0

    lax.fori_loop(0, NY, transpose_x, 0)

    def exchange(i, zs, zss, zr, zrs):
        return [
            remote(zss, zrs, z_sem.at[i, 0], z_sem.at[i, 1], h_peer),
            remote(zs, zr, z_sem.at[i, 2], z_sem.at[i, 3], h_peer),
        ]

    zx_h = exchange(0, zsh, zssh, zrh, zrsh)
    zx_a = exchange(1, zsa, zssa, zra, zrsa)

    def sum_y(copies, n, off, send, ss_send, recv, ss_recv, zs, zss, zx):
        wait(copies)
        value = send[y].astype(F32)
        total = ss_send[y]
        for j in range(1, NY):
            t = lax.rem(y + j, NY)
            value = value + recv[t].astype(F32)
            total = total + ss_recv[t]
        zs[...] = value.astype(BF16)
        zss[...] = total
        start(zx)
        lg[off : off + n, :] = value

    sum_y(rs_h, HROWS, 0, ysh, ssh, yrh, srh, zsh, zssh, zx_h)
    sum_y(rs_a, AROWS, HROWS, ysa, ssa, yra, sra, zsa, zssa, zx_a)

    def column(row_value):
        return jnp.transpose(jnp.broadcast_to(row_value, (128, 128)))

    def row_form(col):
        return jnp.transpose(jnp.broadcast_to(col, (128, 128)))[0:1, :]

    st_z = [remote(stz.at[zl], stz.at[zl], sz_sem.at[0, j], sz_sem.at[1, j], w) for j, w in z_peers]
    st_p = [remote(stp.at[y, x], stp.at[y, x], sp_sem.at[0, i, j], sp_sem.at[1, i, j], w) for i, j, w in plane]
    st_c = [remote(stc.at[core], stc.at[core], sc_sem.at[0], sc_sem.at[1], c_peer)]

    def gather_y(buf, sem):
        return [remote(buf.at[y], buf.at[y], sem.at[0, j], sem.at[1, j], at(y_=t)) for j, t in y_peers]

    e_y, s_y = gather_y(eb, e_sem), gather_y(sc, a_sem)

    wait(zx_h)
    lg[0:HROWS, :] = lg[0:HROWS, :] + zrh[...].astype(F32)
    wait(zx_a)
    lg[HROWS:128, :] = lg[HROWS:128, :] + zra[...].astype(F32)
    scale_row = lax.rsqrt((zssh[...] + zssa[...] + zrsh[...] + zrsa[...]) / D + EPS)
    scale = column(scale_row[0:1, :])
    value = lg[...] * jnp.concatenate([scale, scale], axis=1)
    top_l = jnp.max(value, axis=1, keepdims=True)
    ex = jnp.exp(value - top_l)
    m_row = row_form(top_l)
    stc[core, 0:1, :] = m_row
    stc[core, 1:2, :] = row_form(jnp.sum(ex, axis=1, keepdims=True))
    start(st_c)
    sc[y, 0:1, :] = m_row
    sc[y, 1:2, :] = scale_row
    eb[y] = ex.astype(BF16)

    def join(parts):
        m = parts[0][0:1, :]
        for part_j in parts[1:]:
            m = jnp.maximum(m, part_j[0:1, :])
        sums = parts[0][1:2, :] * jnp.exp(parts[0][0:1, :] - m)
        for part_j in parts[1:]:
            sums = sums + part_j[1:2, :] * jnp.exp(part_j[0:1, :] - m)
        return m, sums

    wait(st_c)
    m_c, sum_c = join([stc[0], stc[1]])
    stz[zl, 0:1, :] = m_c
    stz[zl, 1:2, :] = sum_c
    start(st_z)
    start(s_y)
    start(e_y)
    wait(st_z)
    m_z, sum_z = join([stz[j] for j in range(NZL)])
    stp[y, x, 0:1, :] = m_z
    stp[y, x, 1:2, :] = sum_z
    start(st_p)

    labels = (lax.broadcasted_iota(jnp.int32, (1, COLS), 1) + rep * COLS).astype(F32)
    wait(e_y)
    wait(s_y)
    wait(st_p)

    def deltas(c, _):
        m_all, sum_all = join([stp[c, i] for i in range(NX)])
        s = column(jnp.exp(sc[c, 0:1, :] - m_all) / sum_all)
        r = column(sc[c, 1:2, :])
        t = tcol[c]
        t2 = jnp.concatenate([t, t], axis=1)
        p = eb[c].astype(F32) * jnp.concatenate([s, s], axis=1)
        delta = jnp.where(t2 >= 0.0, p - jnp.where(t2 == labels, 1.0, 0.0), 0.0)
        delta = delta * jnp.concatenate([r, r], axis=1)
        dd[pl.ds(pl.multiple_of(c * 128, 128), 128), :] = delta.astype(BF16)
        return 0

    lax.fori_loop(0, NY, deltas, 0)

    def update(b, _):
        rows = pl.ds(pl.multiple_of(b * 256, 256), 256)
        grad = dot(xt[rows, :], dd[...])
        g = gcol[rows, :] * LEARN_RATE
        w_out[rows, :] = wv[rows, :] - jnp.concatenate([g, g], axis=1) * grad
        return 0

    lax.fori_loop(0, 4, update, 0)


def on_device(queries, cache_keys, cache_values, page_table, lengths, history, norm_gain, draft_weight, targets, accepted):
    vmem = pl.BlockSpec(memory_space=pltpu.VMEM)
    smem = pltpu.SMEM
    hbm = pl.BlockSpec(memory_space=pl.ANY)
    V = pltpu.VMEM
    dma = pltpu.SemaphoreType.DMA
    attended, new_weight = pl.pallas_call(
        body,
        out_shape=(
            V((1, STEPS, FEAT), BF16),
            V((FEAT, COLS), F32),
        ),
        in_specs=[hbm] * 4 + [pl.BlockSpec(memory_space=pltpu.SMEM)] + [hbm] * 5,
        out_specs=(vmem, vmem),
        scratch_shapes=[
            smem((1, 16), jnp.int32),
            V((12, FEAT), BF16), V((1, FEAT), F32), V((16, 64), jnp.int32), V((1, 64), jnp.int32),
            V((STEPS, 2048), BF16), V((1024, HD), BF16), V((1024, HD), BF16), V((FEAT, COLS), F32),
            V((64, HD), F32), V((64, HD), F32), V((40, HD), F32), V((40, HD), F32), V((STEPS, FEAT), F32),
            V((NC, NZL, 8, FEAT), BF16), V((NC, NZL, 4, FEAT), BF16), V((NC, NZL, 4, FEAT), BF16),
            V((4, 8, FEAT), F32), V((NY, 128, FEAT), BF16), V((FEAT, 1024), BF16),
            V((FEAT, COLS), BF16), V((FEAT, COLS), BF16), V((FEAT, 128), F32), V((768, COLS), F32),
            V((128, 128), F32), V((128, 128), F32), V((16, 64), F32), V((NY, 128, 128), F32),
            V((NY, HROWS, COLS), BF16), V((NY, AROWS, COLS), BF16), V((NY, HROWS, COLS), BF16), V((NY, AROWS, COLS), BF16),
            V((NY, 1, 128), F32), V((NY, 1, 128), F32), V((NY, 1, 128), F32), V((NY, 1, 128), F32),
            V((HROWS, COLS), BF16), V((AROWS, COLS), BF16), V((HROWS, COLS), BF16), V((AROWS, COLS), BF16),
            V((1, 128), F32), V((1, 128), F32), V((1, 128), F32), V((1, 128), F32),
            V((128, COLS), F32), V((NZL, 2, 128), F32), V((NY, NX, 2, 128), F32), V((2, 2, 128), F32),
            V((NY, 128, COLS), BF16), V((NY, 2, 128), F32), V((1024, COLS), BF16),
            dma((9,)), dma((2,)), dma((3, 2, 8)), dma((3, 2, 2, 4)), dma((3, 2, 2, 4)), dma((2, 4, 8)), dma((2, 4)),
            dma((2, 8)), dma((2, 4, 8)), dma((2,)), dma((2, 8)), dma((2, 8)),
        ],
        compiler_params=pltpu.CompilerParams(collective_id=0, has_side_effects=True, vmem_limit_bytes=67043328 - 1280 * 1024),
        name="decode_draft_step",
    )(
        queries,
        cache_keys.reshape(1024, HD),
        cache_values.reshape(1024, HD),
        page_table.reshape(1, 16),
        lengths,
        history.reshape(12, FEAT),
        norm_gain.reshape(1, FEAT),
        draft_weight,
        targets.T,
        accepted.reshape(1, 64),
    )
    return attended, new_weight


def solution(mesh):
    return jax.shard_map(
        on_device,
        mesh=mesh,
        in_specs=(
            P("rep", None, None),
            P("rep", "tp", None, None, None),
            P("rep", "tp", None, None, None),
            P("rep", "tp", None),
            P("rep"),
            P("rep", None, "tp"),
            P("tp"),
            P("tp", "rep"),
            P(),
            P(),
        ),
        out_specs=(P("rep", None, "tp"), P("tp", "rep")),
        check_vma=False,
    )
```

```python
import jax
import jax.numpy as jnp
from jax import lax
from jax.experimental import pallas as pl
from jax.experimental.pallas import tpu as pltpu
from jax.sharding import PartitionSpec as P

NX, NCORE, NY, NZL = 4, 2, 8, 8
NC = NX * NCORE
FEAT = 1024
COLS = 256
HEADS = 8
STEPS = 4
HD = 128
D = 16384
LEARN_RATE = 0.5
EPS = 1e-5
F32 = jnp.float32
BF16 = jnp.bfloat16
HROWS, AROWS = 96, 32


def remote(src, dst, send, recv, where):
    return pltpu.make_async_remote_copy(
        src_ref=src,
        dst_ref=dst,
        send_sem=send,
        recv_sem=recv,
        device_id=where,
        device_id_type=pl.DeviceIdType.MESH,
    )


def split_bf16(value):
    high = value.astype(BF16)
    return high, (value - high.astype(F32)).astype(BF16)


def dot(a, b):
    return jnp.dot(a, b, preferred_element_type=F32)


def body(
    q_hbm, k_hbm, v_hbm, table_hbm, length, hist_hbm, gain_hbm, w_hbm, targets_hbm, accepted_hbm,
    att_out, w_out,
    table, hist, gain, targets, accepted,
    qv, kv, vv, wv, q32, part, px_send, px_recv, blk,
    r8, r4, ra, f4, xr, xt, whi, wlo, gcol, pacc,
    tmp, tmp2, tk, tcol,
    ysh, ysa, yrh, yra, ssh, ssa, srh, sra,
    zsh, zsa, zrh, zra, zssh, zssa, zrsh, zrsa,
    lg, stz, stp, stc, eb, sc, dd,
    load_sem, px_sem, gz_sem, gx_sem, gc_sem, y_sem, z_sem, sz_sem, sp_sem, sc_sem, e_sem,
):
    rep = lax.axis_index("rep")
    tp = lax.axis_index("tp")
    core = lax.rem(rep, 2)
    x = lax.rem(rep // 2, NX)
    zl = rep // NC
    zh = lax.rem(tp, 2)
    y = tp // 2
    cc = core * NX + x
    own_base = core * NX
    other_base = (1 - core) * NX

    def at(zl_=None, x_=None, core_=None, y_=None, zh_=None):
        r = ((zl if zl_ is None else zl_) * NX + (x if x_ is None else x_)) * NCORE + (core if core_ is None else core_)
        t = (y if y_ is None else y_) * 2 + (zh if zh_ is None else zh_)
        return (r, t)

    half = zl // 4
    near = [half * 4 + lax.rem(lax.rem(zl, 4) + j, 4) for j in range(1, 4)]
    far = [(1 - half) * 4 + lax.rem(lax.rem(zl, 4) + j, 4) for j in range(4)]
    z_peers = [(j, at(zl_=t)) for j, t in enumerate(near + far)]
    x_peers = [(j, at(x_=lax.rem(x + j, NX))) for j in range(1, NX)]
    plane = [
        (i, j, at(x_=lax.rem(x + i, NX), y_=lax.rem(y + j, NY)))
        for i in range(NX)
        for j in range(NY)
        if i or j
    ]
    c_peer = at(core_=1 - core)
    y_half = y // 4
    y_near = [y_half * 4 + lax.rem(lax.rem(y, 4) + j, 4) for j in range(1, 4)]
    y_far = [(1 - y_half) * 4 + lax.rem(lax.rem(y, 4) + j, 4) for j in range(4)]
    y_peers = list(enumerate(y_near + y_far))
    h_peer = at(zh_=1 - zh)

    barrier = pltpu.get_barrier_semaphore()
    everyone = [h_peer] + [w for _, w in z_peers] + [w for _, _, w in plane] + [c_peer]
    for where in everyone:
        pl.semaphore_signal(barrier, inc=1, device_id=where, device_id_type=pl.DeviceIdType.MESH)

    group = tp // 2
    loads = [
        pltpu.make_async_copy(src, dst, load_sem.at[i])
        for i, (src, dst) in enumerate(
            [
                (q_hbm.at[0, :, pl.ds(pl.multiple_of(group * 2048, 2048), 2048)], qv),
                (k_hbm, kv),
                (table_hbm, table),
                (v_hbm, vv),
                (hist_hbm, hist),
                (gain_hbm, gain),
                (w_hbm, wv),
                (targets_hbm, targets),
                (accepted_hbm, accepted),
            ]
        )
    ]
    for load in loads:
        load.start()

    def start(copies):
        for copy in copies:
            copy.start()

    def wait(copies):
        for copy in copies:
            copy.wait()

    tmp[...] = jnp.zeros_like(tmp)
    tmp2[...] = jnp.zeros_like(tmp2)

    wait(loads[0:3])
    lane = lax.broadcasted_iota(jnp.int32, (8, 1024), 1)
    page = lane // 64
    logical = jnp.zeros((8, 1024), jnp.int32)
    for j in range(16):
        logical = jnp.where(page == table[0, j], j, logical)
    position = (logical * 2 + zh) * 64 + lax.rem(lane, 64)
    row = lax.broadcasted_iota(jnp.int32, (8, 1024), 0)
    valid8 = position <= length[0] - STEPS + lax.rem(row, STEPS)
    bias = jnp.where(valid8, 0.0, -1e30)
    for h in range(16):
        q32[h * STEPS : (h + 1) * STEPS, :] = qv[:, h * HD : (h + 1) * HD].astype(F32)
    scores = lax.dot_general(
        q32[...].astype(BF16), kv[...], (((1,), (1,)), ((), ())), preferred_element_type=F32
    ) * (HD ** -0.5)
    valid = jnp.concatenate([bias] * 8, axis=0) == 0.0
    top = jnp.max(jnp.where(valid, scores, -1e30), axis=-1, keepdims=True)
    expo = jnp.where(valid, jnp.exp(scores - top), 0.0)
    total = jnp.sum(expo, axis=-1, keepdims=True)
    e_high, e_low = split_bf16(expo)
    tmp[0:64, :] = jnp.broadcast_to(top, (64, 128))
    tmp[64:128, :] = jnp.broadcast_to(total, (64, 128))
    stat_rows = jnp.transpose(tmp[...])
    loads[3].wait()
    part[...] = dot(e_high, vv[...]) + dot(e_low, vv[...])
    other = pl.multiple_of((1 - zh) * 32, 32)
    px_send[0:32, :] = part[pl.ds(other, 32), :]
    px_send[32:40, :] = stat_rows[0:8, :]

    loads[4].wait()
    h32 = hist[...].astype(F32)
    r8[cc, zl] = h32[0:8].astype(BF16)
    r4[cc, zl] = h32[8:12].astype(BF16)

    pl.semaphore_wait(barrier, len(everyone))
    px = remote(px_send, px_recv, px_sem.at[0], px_sem.at[1], h_peer)
    px.start()

    across = (1 - half) * 4 + lax.rem(zl, 4)

    def gather(buf, i, relay):
        def send(k, j, where):
            return remote(buf.at[cc, k], buf.at[cc, k], gz_sem.at[i, 0, j], gz_sem.at[i, 1, j], where)

        z = [send(zl, j, where) for j, where in z_peers]
        if relay:
            z = z[0:4] + [send(across, j + 4, where) for j, where in z_peers[0:3]]

        def piece(k, h):
            return buf.at[k, pl.ds(h * 4, 4)]

        xs, cs = [], []
        for slot, h in ((0, half), (1, 1 - half)):
            xs.append(
                [
                    remote(piece(cc, h), piece(cc, h), gx_sem.at[i, slot, 0, j], gx_sem.at[i, slot, 1, j], where)
                    for j, where in x_peers
                ]
            )
            one = []
            for j in range(NX):
                k = own_base + lax.rem(x + j, NX)
                one.append(remote(piece(k, h), piece(k, h), gc_sem.at[i, slot, 0, j], gc_sem.at[i, slot, 1, j], c_peer))
            cs.append(one)
        return z[0:3], z[3:4] if relay else z[3:7], xs, cs, z[4:7]

    g8, g4, ga = gather(r8, 0, True), gather(r4, 1, True), gather(ra, 2, False)
    start(g8[0] + g4[0] + g8[1] + g4[1])

    wait(loads[5:7])

    def make_w(b, _):
        rows = pl.ds(pl.multiple_of(b * 128, 128), 128)
        g = jnp.transpose(jnp.broadcast_to(gain[0:1, rows], (128, 128)))
        gcol[rows, :] = g
        w = wv[rows, :] * jnp.concatenate([g, g], axis=1)
        high, low = split_bf16(w)
        whi[rows, :] = high
        wlo[rows, :] = low
        return 0

    lax.fori_loop(0, 8, make_w, 0)

    wait(g8[0] + g4[0])
    start(g8[2][0] + g4[2][0])
    wait(g8[1] + g4[1])
    start(g8[4] + g4[4])

    tmp[0:64, :] = jnp.broadcast_to(stat_rows[0:1, :], (64, 128))
    px.wait()
    tmp[64:128, :] = jnp.broadcast_to(px_recv[32:33, :], (64, 128))
    tmp[...] = jnp.transpose(tmp[...])
    mine = pl.multiple_of(zh * 32, 32)
    top_a = tmp[pl.ds(mine, 32), 0:1]
    sum_a = tmp[pl.ds(mine + 64, 32), 0:1]
    top_b = tmp[pl.ds(mine, 32), 64:65]
    sum_b = tmp[pl.ds(mine + 64, 32), 64:65]
    top_ab = jnp.maximum(top_a, top_b)
    left = jnp.exp(top_a - top_ab)
    right = jnp.exp(top_b - top_ab)
    joined = (part[pl.ds(mine, 32), :] * left + px_recv[0:32, :] * right) / (sum_a * left + sum_b * right)
    part[0:32, :] = joined
    for h in range(HEADS):
        blk[:, h * HD : (h + 1) * HD] = part[h * STEPS : (h + 1) * STEPS, :]
    own = blk[...].astype(BF16)
    ra[cc, zl] = own
    start(ga[0] + ga[1])
    att_out[0] = own

    wait(g8[4] + g4[4])
    start(g8[2][1] + g4[2][1])

    wait(loads[7:9])
    ii = lax.broadcasted_iota(jnp.int32, (16, 64), 0)
    tk[...] = jnp.where(ii < accepted[...], targets[...], -1).astype(F32)
    rho = lax.broadcasted_iota(jnp.int32, (128, 64), 0)
    rep_lane = lax.broadcasted_iota(jnp.int32, (128, 64), 1)
    zl_of = jnp.where(rho < 64, rho // 8, jnp.where(rho < 96, (rho - 64) // 4, (rho - 96) // 4))
    rho16 = lax.broadcasted_iota(jnp.int32, (128, 16), 0)
    lane16 = lax.broadcasted_iota(jnp.int32, (128, 16), 1)
    i_of = jnp.where(rho16 < 64, 4 + lax.rem(rho16, 8), jnp.where(rho16 < 96, 12, 0) + lax.rem(rho16, 4))

    def target_cols(c, _):
        pick = (rep_lane == zl_of * NC + lax.rem(c, NX) * NCORE + c // NX).astype(F32)
        rows = lax.dot_general(
            pick, tk[...], (((1,), (1,)), ((), ())), precision=lax.Precision.HIGHEST, preferred_element_type=F32
        )
        col = jnp.sum(jnp.where(lane16 == i_of, rows, 0.0), axis=1, keepdims=True)
        tcol[c] = jnp.broadcast_to(col, (128, 128))
        return 0

    lax.fori_loop(0, NY, target_cols, 0)

    wait(g8[2][0] + g4[2][0])
    start(g8[3][0] + g4[3][0])
    wait(g8[2][1] + g4[2][1])
    start(g8[3][1] + g4[3][1])

    def narrow_rows(buf, c):
        for j in range(4):
            f4[j, 0:4, :] = buf[c, 2 * j].astype(F32)
            f4[j, 4:8, :] = buf[c, 2 * j + 1].astype(F32)
        return f4[...].reshape(32, FEAT)

    def prep_h(c, _):
        v8 = r8[c].astype(F32).reshape(64, FEAT)
        v4 = narrow_rows(r4, c)
        xr[c, 0:64, :] = v8.astype(BF16)
        xr[c, 64:96, :] = v4.astype(BF16)
        tmp[0:64, :] = jnp.broadcast_to(jnp.sum(v8 * v8, axis=1, keepdims=True), (64, 128))
        tmp[64:96, :] = jnp.broadcast_to(jnp.sum(v4 * v4, axis=1, keepdims=True), (32, 128))
        tmp[96:128, :] = jnp.zeros((32, 128), F32)
        ssh[c] = jnp.transpose(tmp[...])[0:1, :]
        return 0

    def logits_h(base):
        lax.fori_loop(0, NX, lambda k, z: prep_h(base + k, z), 0)
        rows_h = xr[pl.ds(base, NX), 0:HROWS, :].reshape(NX * HROWS, FEAT)
        pacc[...] = dot(rows_h, whi[...]) + dot(rows_h, wlo[...])

        def pack_h(k, _):
            ysh[base + k] = pacc[pl.ds(pl.multiple_of(k * HROWS, 32), HROWS), :].astype(BF16)
            return 0

        lax.fori_loop(0, NX, pack_h, 0)

    def scatter(i, send, ss_send, recv, ss_recv):
        copies = []
        for j, t in y_peers:
            where = at(y_=t)
            copies.append(remote(ss_send.at[t], ss_recv.at[y], y_sem.at[i, 0, j], y_sem.at[i, 1, j], where))
            copies.append(remote(send.at[t], recv.at[y], y_sem.at[i, 2, j], y_sem.at[i, 3, j], where))
        return copies

    rs_h = scatter(0, ysh, ssh, yrh, srh)
    rs_a = scatter(1, ysa, ssa, yra, sra)
    rs_near, rs_far = rs_h[0:6], rs_h[6:14]
    near_first = y_half == core
    logits_h(own_base)

    @pl.when(near_first)
    def _():
        start(rs_near)

    @pl.when(jnp.logical_not(near_first))
    def _():
        start(rs_far)

    wait(g8[3][0] + g4[3][0] + g8[3][1] + g4[3][1])
    logits_h(other_base)

    @pl.when(near_first)
    def _():
        start(rs_far)

    @pl.when(jnp.logical_not(near_first))
    def _():
        start(rs_near)

    wait(ga[0])
    start(ga[2][0])
    wait(ga[1])
    start(ga[2][1])
    wait(ga[2][0] + ga[2][1])
    start(ga[3][0] + ga[3][1])
    wait(ga[3][0] + ga[3][1])

    def prep_a(c, _):
        v4 = narrow_rows(ra, c)
        xr[c, 96:128, :] = v4.astype(BF16)
        tmp2[96:128, :] = jnp.broadcast_to(jnp.sum(v4 * v4, axis=1, keepdims=True), (32, 128))
        ssa[c] = jnp.transpose(tmp2[...])[0:1, :]
        return 0

    lax.fori_loop(0, NY, prep_a, 0)
    rows_a = xr[:, HROWS:128, :].reshape(NY * AROWS, FEAT)
    pacc[0:256, :] = dot(rows_a, whi[...]) + dot(rows_a, wlo[...])

    def pack_a(c, _):
        ysa[c] = pacc[pl.ds(pl.multiple_of(c * AROWS, 32), AROWS), :].astype(BF16)
        return 0

    lax.fori_loop(0, NY, pack_a, 0)
    start(rs_a)

    def transpose_x(c, _):
        lanes = pl.ds(pl.multiple_of(c * 128, 128), 128)
        xt[:, lanes] = jnp.transpose(xr[c].astype(F32)).astype(BF16)
        return 0

    lax.fori_loop(0, NY, transpose_x, 0)

    def exchange(i, zs, zss, zr, zrs):
        return [
            remote(zss, zrs, z_sem.at[i, 0], z_sem.at[i, 1], h_peer),
            remote(zs, zr, z_sem.at[i, 2], z_sem.at[i, 3], h_peer),
        ]

    zx_h = exchange(0, zsh, zssh, zrh, zrsh)
    zx_a = exchange(1, zsa, zssa, zra, zrsa)

    def sum_y(copies, n, off, send, ss_send, recv, ss_recv, zs, zss, zx):
        wait(copies)
        value = send[y].astype(F32)
        total = ss_send[y]
        for j in range(1, NY):
            t = lax.rem(y + j, NY)
            value = value + recv[t].astype(F32)
            total = total + ss_recv[t]
        zs[...] = value.astype(BF16)
        zss[...] = total
        start(zx)
        lg[off : off + n, :] = value

    sum_y(rs_h, HROWS, 0, ysh, ssh, yrh, srh, zsh, zssh, zx_h)
    sum_y(rs_a, AROWS, HROWS, ysa, ssa, yra, sra, zsa, zssa, zx_a)

    def column(row_value):
        return jnp.transpose(jnp.broadcast_to(row_value, (128, 128)))

    def row_form(col):
        return jnp.transpose(jnp.broadcast_to(col, (128, 128)))[0:1, :]

    st_z = [remote(stz.at[zl], stz.at[zl], sz_sem.at[0, j], sz_sem.at[1, j], w) for j, w in z_peers]
    st_p = [remote(stp.at[y, x], stp.at[y, x], sp_sem.at[0, i, j], sp_sem.at[1, i, j], w) for i, j, w in plane]
    st_c = [remote(stc.at[core], stc.at[core], sc_sem.at[0], sc_sem.at[1], c_peer)]

    def gather_y(buf, sem):
        return [remote(buf.at[y], buf.at[y], sem.at[0, j], sem.at[1, j], at(y_=t)) for j, t in y_peers]

    e_y = gather_y(eb, e_sem)

    wait(zx_h)
    lg[0:HROWS, :] = lg[0:HROWS, :] + zrh[...].astype(F32)
    wait(zx_a)
    lg[HROWS:128, :] = lg[HROWS:128, :] + zra[...].astype(F32)
    scale_row = lax.rsqrt((zssh[...] + zssa[...] + zrsh[...] + zrsa[...]) / D + EPS)
    scale = column(scale_row[0:1, :])
    value = lg[...] * jnp.concatenate([scale, scale], axis=1)
    top_l = jnp.max(value, axis=1, keepdims=True)
    ex = jnp.exp(value - top_l)
    m_row = row_form(top_l)
    stp[y, x, 0:1, :] = m_row
    stp[y, x, 1:2, :] = row_form(jnp.sum(ex, axis=1, keepdims=True))
    stp[y, x, 2:3, :] = scale_row
    stp[y, x, 3:4, :] = jnp.zeros((1, 128), F32)
    start(st_p)
    eb[y] = ex.astype(BF16)
    start(e_y)

    def join(parts):
        m = parts[0][0]
        for part_j in parts[1:]:
            m = jnp.maximum(m, part_j[0])
        sums = parts[0][1] * jnp.exp(parts[0][0] - m)
        for part_j in parts[1:]:
            sums = sums + part_j[1] * jnp.exp(part_j[0] - m)
        return m, sums

    wait(st_p)
    for c in range(NY):
        m_x, sum_x = join([(stp[c, i, 0:1, :], stp[c, i, 1:2, :]) for i in range(NX)])
        stc[core, 0, c : c + 1, :] = m_x
        stc[core, 1, c : c + 1, :] = sum_x
        sc[0, c : c + 1, :] = stp[c, x, 0:1, :]
    start(st_c)
    wait(st_c)
    m_c, sum_c = join([(stc[j, 0], stc[j, 1]) for j in range(NCORE)])
    stz[zl, 0] = m_c
    stz[zl, 1] = sum_c
    start(st_z)
    wait(st_z)
    m_all, sum_all = join([(stz[j, 0], stz[j, 1]) for j in range(NZL)])
    sc[1] = jnp.exp(sc[0] - m_all) / sum_all

    labels = (lax.broadcasted_iota(jnp.int32, (1, COLS), 1) + rep * COLS).astype(F32)
    wait(e_y)

    def deltas(c, _):
        s = column(sc[1, pl.ds(c, 1), :])
        r = column(stp[c, 0, 2:3, :])
        t = tcol[c]
        t2 = jnp.concatenate([t, t], axis=1)
        p = eb[c].astype(F32) * jnp.concatenate([s, s], axis=1)
        delta = jnp.where(t2 >= 0.0, p - jnp.where(t2 == labels, 1.0, 0.0), 0.0)
        delta = delta * jnp.concatenate([r, r], axis=1)
        dd[pl.ds(pl.multiple_of(c * 128, 128), 128), :] = delta.astype(BF16)
        return 0

    lax.fori_loop(0, NY, deltas, 0)

    def update(b, _):
        rows = pl.ds(pl.multiple_of(b * 256, 256), 256)
        grad = dot(xt[rows, :], dd[...])
        g = gcol[rows, :] * LEARN_RATE
        w_out[rows, :] = wv[rows, :] - jnp.concatenate([g, g], axis=1) * grad
        return 0

    lax.fori_loop(0, 4, update, 0)


def on_device(queries, cache_keys, cache_values, page_table, lengths, history, norm_gain, draft_weight, targets, accepted):
    vmem = pl.BlockSpec(memory_space=pltpu.VMEM)
    smem = pltpu.SMEM
    hbm = pl.BlockSpec(memory_space=pl.ANY)
    V = pltpu.VMEM
    dma = pltpu.SemaphoreType.DMA
    attended, new_weight = pl.pallas_call(
        body,
        out_shape=(
            V((1, STEPS, FEAT), BF16),
            V((FEAT, COLS), F32),
        ),
        in_specs=[hbm] * 4 + [pl.BlockSpec(memory_space=pltpu.SMEM)] + [hbm] * 5,
        out_specs=(vmem, vmem),
        scratch_shapes=[
            smem((1, 16), jnp.int32),
            V((12, FEAT), BF16), V((1, FEAT), F32), V((16, 64), jnp.int32), V((1, 64), jnp.int32),
            V((STEPS, 2048), BF16), V((1024, HD), BF16), V((1024, HD), BF16), V((FEAT, COLS), F32),
            V((64, HD), F32), V((64, HD), F32), V((40, HD), F32), V((40, HD), F32), V((STEPS, FEAT), F32),
            V((NC, NZL, 8, FEAT), BF16), V((NC, NZL, 4, FEAT), BF16), V((NC, NZL, 4, FEAT), BF16),
            V((4, 8, FEAT), F32), V((NY, 128, FEAT), BF16), V((FEAT, 1024), BF16),
            V((FEAT, COLS), BF16), V((FEAT, COLS), BF16), V((FEAT, 128), F32), V((NX * HROWS, COLS), F32),
            V((128, 128), F32), V((128, 128), F32), V((16, 64), F32), V((NY, 128, 128), F32),
            V((NY, HROWS, COLS), BF16), V((NY, AROWS, COLS), BF16), V((NY, HROWS, COLS), BF16), V((NY, AROWS, COLS), BF16),
            V((NY, 1, 128), F32), V((NY, 1, 128), F32), V((NY, 1, 128), F32), V((NY, 1, 128), F32),
            V((HROWS, COLS), BF16), V((AROWS, COLS), BF16), V((HROWS, COLS), BF16), V((AROWS, COLS), BF16),
            V((1, 128), F32), V((1, 128), F32), V((1, 128), F32), V((1, 128), F32),
            V((128, COLS), F32), V((NZL, 2, NY, 128), F32), V((NY, NX, 4, 128), F32), V((NCORE, 2, NY, 128), F32),
            V((NY, 128, COLS), BF16), V((2, NY, 128), F32), V((1024, COLS), BF16),
            dma((9,)), dma((2,)), dma((3, 2, 8)), dma((3, 2, 2, 4)), dma((3, 2, 2, 4)), dma((2, 4, 8)), dma((2, 4)),
            dma((2, 8)), dma((2, 4, 8)), dma((2,)), dma((2, 8)),
        ],
        compiler_params=pltpu.CompilerParams(collective_id=0, has_side_effects=True, vmem_limit_bytes=67043328 - 1280 * 1024),
        name="decode_draft_step",
    )(
        queries,
        cache_keys.reshape(1024, HD),
        cache_values.reshape(1024, HD),
        page_table.reshape(1, 16),
        lengths,
        history.reshape(12, FEAT),
        norm_gain.reshape(1, FEAT),
        draft_weight,
        targets.T,
        accepted.reshape(1, 64),
    )
    return attended, new_weight


def solution(mesh):
    return jax.shard_map(
        on_device,
        mesh=mesh,
        in_specs=(
            P("rep", None, None),
            P("rep", "tp", None, None, None),
            P("rep", "tp", None, None, None),
            P("rep", "tp", None),
            P("rep"),
            P("rep", None, "tp"),
            P("tp"),
            P("tp", "rep"),
            P(),
            P(),
        ),
        out_specs=(P("rep", None, "tp"), P("tp", "rep")),
        check_vma=False,
    )
```
